32 devices in a mesh: gx: 8 (over y, x, core), gy: 4 (over z).
Axes of the slice: x: 2, y: 2, z: 4, core: 2. Of those that a mesh axis runs over, the one named last changes fastest.
Arguments:
- particle_count: int32 [8, 256, 1024], P(None, ('gx', 'gy')), may hold values from 0 to 12
- drag_coeff: float32 [8, 256, 1024], P(None, ('gx', 'gy')), may hold values from 0.05 to 2
- particle_velocity: float32 [3, 8, 256, 1024], P(None, None, ('gx', 'gy')), may hold values from -6 to 6
- fluid_velocity: float32 [3, 8, 256, 1024], P(None, None, 'gy', 'gx'), may hold values from -6 to 6
Outputs:
- pressure: float32 [8, 256, 1024], P(None, 'gy', 'gx')
- new_velocity: float32 [3, 8, 256, 1024], P(None, None, ('gx', 'gy'))
- pressure_gradient: float32 [3, 8, 256, 1024], P(None, None, ('gx', 'gy'))
The draws below stay inside these ranges and needn't reach their ends.
All inputs are finite; a program needn't handle non-finite values.
Results may differ from the reference program's by a relative error of at most 0.00002.
Values sent between devices are 32-bit elements; how exact they have to be, the bound alone decides.
A program may use at most 64 MiB of HBM per device.

```python
import math
import jax
import jax.numpy as jnp

NZ = 8
SWEEPS = 8
NX = 256
NY = 1024


def place_ends(result, rng, least, top_value):
    extent = result.shape
    spot = [jax.random.randint(jax.random.fold_in(rng, axis), (), 0, extent[axis]) for axis in range(len(extent))]
    result = result.at[tuple(spot)].set(least)
    longest = extent.index(max(extent))
    spot[longest] = (spot[longest] + 1) % extent[longest]
    return result.at[tuple(spot)].set(top_value)


def levels(own_key, dims, shards, low, high):
    def one(axis_at, blocks):
        steps = jax.random.uniform(jax.random.fold_in(jax.random.fold_in(own_key, 6), axis_at), (blocks,), jnp.float32, low / len(shards), high / len(shards))
        return jnp.repeat(jnp.exp(steps), dims[axis_at] // blocks).reshape((-1,) + (1,) * (len(dims) - axis_at - 1))

    gain = one(*shards[0])
    for cut in shards[1:]:
        gain = gain * one(*cut)
    return gain


def gaussian(key, dims, width, reach, split=(), held_as=jnp.bfloat16):
    level = levels(key, dims, split, -0.22, 0.18) if split else 1.0
    entries = jax.random.normal(key, dims, jnp.float32) * width * level
    return jnp.minimum(jnp.maximum(entries, -reach), reach).astype(held_as)


def setup_inputs(seed: int = 0) -> dict:
    arg_keys = jax.random.split(jax.random.key(seed), 5)
    particle_count = place_ends(jax.random.randint(arg_keys[0], (NZ, NX, NY), 0, 13), jax.random.fold_in(arg_keys[0], 1), 0, 12).astype(jnp.int32)
    drag_coeff = jnp.clip(jnp.exp(math.log(2.0) - 3.6888794 * jax.random.uniform(arg_keys[1], (NZ, NX, NY), jnp.float32) ** levels(arg_keys[1], (NZ, NX, NY), ((1, 32),), -0.2, 0.2)), 0.05, 2.0)
    particle_velocity = gaussian(arg_keys[2], (3, NZ, NX, NY), 1.0, 6.0, ((2, 32),), jnp.float32)
    fluid_velocity = gaussian(arg_keys[3], (3, NZ, NX, NY), 1.0, 6.0, ((2, 4), (3, 8)), jnp.float32)
    return {"particle_count": particle_count, "drag_coeff": drag_coeff, "particle_velocity": particle_velocity, "fluid_velocity": fluid_velocity}


particle_volume = 0.05
time_step = 0.5
viscosity = 0.1


def pad_depth(values):
    widths = [(0, 0)] * (values.ndim - 3) + [(1, 1), (0, 0), (0, 0)]
    return jnp.pad(values, widths)


def pad_plane(values):
    widths = [(0, 0)] * (values.ndim - 2) + [(1, 1), (1, 1)]
    return jnp.pad(values, widths)


def middle(values):
    return values[..., 1:-1, 1:-1, 1:-1]


def neighbour(values, which):
    if which == 0:
        return values[..., 2:, 1:-1, 1:-1]
    if which == 1:
        return values[..., :-2, 1:-1, 1:-1]
    if which == 2:
        return values[..., 1:-1, 2:, 1:-1]
    if which == 3:
        return values[..., 1:-1, :-2, 1:-1]
    if which == 4:
        return values[..., 1:-1, 1:-1, 2:]
    return values[..., 1:-1, 1:-1, :-2]


def face_weights(voids_wide):
    padded = pad_depth(voids_wide)
    centre = middle(padded)
    weights = jnp.stack([0.5 * (centre + neighbour(padded, which)) for which in range(6)])
    weight_sum = weights[0]
    for which in range(1, 6):
        weight_sum = weight_sum + weights[which]
    return weights, weight_sum


def momentum(velocity_wide, weights, voids, drag, drag_force):
    padded = pad_depth(velocity_wide)
    centre = middle(padded)
    diffusion = jnp.zeros_like(centre)
    for which in range(6):
        diffusion = diffusion + weights[which][None] * (neighbour(padded, which) - centre)
    return (voids[None] * centre + time_step * viscosity * diffusion + time_step * drag_force) / (voids[None] + time_step * drag[None])


def divergence(flux_wide):
    first = flux_wide[0][:, 2:, 1:-1] - flux_wide[0][:, :-2, 1:-1]
    second = flux_wide[1][:, 1:-1, 2:] - flux_wide[1][:, 1:-1, :-2]
    normal = pad_depth(flux_wide[2])[:, 1:-1, 1:-1]
    third = normal[2:] - normal[:-2]
    return 0.5 * (first + second + third) / time_step


def jacobi_sweep(pressure_wide, weights, weight_sum, source):
    padded = pad_depth(pressure_wide)
    total = weights[0] * neighbour(padded, 0)
    for which in range(1, 6):
        total = total + weights[which] * neighbour(padded, which)
    return (total - source) / weight_sum


def gradient_of(pressure_wide):
    padded = pad_depth(pressure_wide)
    first = 0.5 * (padded[1:-1, 2:, 1:-1] - padded[1:-1, :-2, 1:-1])
    second = 0.5 * (padded[1:-1, 1:-1, 2:] - padded[1:-1, 1:-1, :-2])
    third = 0.5 * (padded[2:, 1:-1, 1:-1] - padded[:-2, 1:-1, 1:-1])
    return jnp.stack([first, second, third])


def reference(particle_count, drag_coeff, particle_velocity, fluid_velocity):
    voids = 1.0 - particle_count.astype(jnp.float32) * particle_volume
    drag_force = drag_coeff[None] * particle_velocity
    weights, weight_sum = face_weights(pad_plane(voids))
    predicted = momentum(pad_plane(fluid_velocity), weights, voids, drag_coeff, drag_force)
    flux = voids[None] * predicted
    source = divergence(pad_plane(flux))
    pressure = (-source) / weight_sum
    for sweep_index in range(SWEEPS - 1):
        pressure = jacobi_sweep(pad_plane(pressure), weights, weight_sum, source)
    slopes = gradient_of(pad_plane(pressure))
    velocity = predicted - time_step * slopes
    return pressure, velocity, slopes
```

```python
import functools

import jax
import jax.numpy as jnp
from jax import lax
from jax.experimental import pallas as pl
from jax.experimental.pallas import tpu as pltpu
from jax.sharding import PartitionSpec as P

SWEEPS = 8
ROUNDS = (4, 4)

particle_volume = 0.05
time_step = 0.5
viscosity = 0.1


def kernel(
    K, G, R, NZ, NY, W,
    count_in, drag_in, pvel_in, fluid_in,
    press_out, vel_out, grad_out,
    fp, z0, z1, u0, u12, cn, dr, pv0, pv12, vo, rh, pred, fl, b, pm, t0, t1, pf, po,
    loc_sem, fh_send, fh_recv, s1_send, s1_recv, s2_send, s2_recv,
    hal_send, hal_recv, pr_send, pr_recv, out_send, out_recv,
):
    H = ROUNDS[0]
    C = G // K
    B = C * K
    x = lax.axis_index("gx")
    k = lax.axis_index("gy")
    place = x * K + k
    has_prev = place > 0
    has_next = place < G * K - 1
    prev_id = {"gx": jnp.where(k > 0, x, jnp.maximum(x - 1, 0)), "gy": lax.rem(k + K - 1, K)}
    next_id = {"gx": jnp.where(k < K - 1, x, jnp.minimum(x + 1, G - 1)), "gy": lax.rem(k + 1, K)}

    def remote(src, dst, ssem, rsem, to):
        return pltpu.make_async_remote_copy(
            src_ref=src, dst_ref=dst, send_sem=ssem, recv_sem=rsem, device_id=to, device_id_type=pl.DeviceIdType.MESH
        )

    rows = R * B

    up = {"gx": x, "gy": lax.rem(k + K - 1, K)}
    down = {"gx": x, "gy": lax.rem(k + 1, K)}
    to_up = remote(fluid_in.at[:, 0:2], fp.at[:, rows + 2:rows + 4], fh_send.at[0], fh_recv.at[0], up)
    to_down = remote(fluid_in.at[:, rows - 2:rows], fp.at[:, 0:2], fh_send.at[1], fh_recv.at[1], down)

    @pl.when(k > 0)
    def _():
        to_up.start()

    @pl.when(k < K - 1)
    def _():
        to_down.start()

    local = [
        pltpu.make_async_copy(fluid_in, fp.at[:, 2:rows + 2], loc_sem.at[0]),
        pltpu.make_async_copy(count_in, cn.at[H:H + R], loc_sem.at[1]),
        pltpu.make_async_copy(drag_in, dr.at[1:R + 1], loc_sem.at[2]),
        pltpu.make_async_copy(pvel_in.at[0], pv0.at[1:R + 1], loc_sem.at[3]),
        pltpu.make_async_copy(pvel_in.at[1:3], pv12, loc_sem.at[4]),
    ]
    for copy in local:
        copy.start()

    halo_up = [
        remote(count_in.at[0:H], cn.at[H + R:2 * H + R], hal_send.at[0], hal_recv.at[0], prev_id),
        remote(drag_in.at[0:1], dr.at[R + 1:R + 2], hal_send.at[1], hal_recv.at[1], prev_id),
        remote(pvel_in.at[0, 0:1], pv0.at[R + 1:R + 2], hal_send.at[2], hal_recv.at[2], prev_id),
    ]
    halo_down = [
        remote(count_in.at[R - H:R], cn.at[0:H], hal_send.at[3], hal_recv.at[3], next_id),
        remote(drag_in.at[R - 1:R], dr.at[0:1], hal_send.at[4], hal_recv.at[4], next_id),
        remote(pvel_in.at[0, R - 1:R], pv0.at[0:1], hal_send.at[5], hal_recv.at[5], next_id),
    ]

    @pl.when(k == 0)
    def _():
        fp[:, 0:2] = jnp.zeros((3, 2, NZ, W), jnp.float32)

    @pl.when(k == K - 1)
    def _():
        fp[:, rows + 2:rows + 4] = jnp.zeros((3, 2, NZ, W), jnp.float32)

    edge = jnp.zeros((H, NZ, NY), jnp.float32)

    @pl.when(jnp.logical_not(has_prev))
    def _():
        b[0:H] = edge
        pm[0:H] = edge

    @pl.when(jnp.logical_not(has_next))
    def _():
        b[H + R:2 * H + R] = edge
        pm[H + R:2 * H + R] = edge

    local[0].wait()

    @pl.when(k < K - 1)
    def _():
        to_up.wait_recv()

    @pl.when(k > 0)
    def _():
        to_down.wait_recv()

    def part0(at):
        return fp.at[0, pl.ds(at * R, R + 4)]

    def part1(at):
        return fp.at[1:3, pl.ds(at * R + 1, R + 2)]

    first = []
    for d in range(1, K):
        j = lax.rem(k + d, K)
        to = {"gx": x, "gy": j}
        pair = []
        for c in range(C):
            n = ((d - 1) * C + c) * 2
            pair.append(remote(part0(c * K + j), z0.at[d - 1, c], s1_send.at[n], s1_recv.at[n], to))
            pair.append(remote(part1(c * K + j), z1.at[d - 1, c], s1_send.at[n + 1], s1_recv.at[n + 1], to))
        for copy in pair:
            copy.start()
        first.append(pair)

    columns = pl.ds(pl.multiple_of(x * W, W), W)
    second = []
    for d in range(K):
        source = lax.rem(k + K - d, K)
        if d > 0:
            for copy in first[d - 1]:
                copy.wait_recv()
        for c in range(C):
            target = source * C + c
            n = (d * C + c) * 2
            src0 = part0(c * K + k) if d == 0 else z0.at[d - 1, c]
            src1 = part1(c * K + k) if d == 0 else z1.at[d - 1, c]
            dst0 = u0.at[:, :, columns]
            dst1 = u12.at[:, :, :, columns]
            to = {"gx": target, "gy": k}
            far0 = remote(src0, dst0, s2_send.at[n], s2_recv.at[2 * x], to)
            far1 = remote(src1, dst1, s2_send.at[n + 1], s2_recv.at[2 * x + 1], to)
            near0 = pltpu.make_async_copy(src0, dst0, s2_recv.at[2 * x])
            near1 = pltpu.make_async_copy(src1, dst1, s2_recv.at[2 * x + 1])

            @pl.when(target != x)
            def _(far0=far0, far1=far1):
                far0.start()
                far1.start()

            @pl.when(target == x)
            def _(near0=near0, near1=near1):
                near0.start()
                near1.start()

            second.append((target, far0, far1))
        if d == 0:
            @pl.when(has_prev)
            def _():
                for copy in halo_up:
                    copy.start()

            @pl.when(has_next)
            def _():
                for copy in halo_down:
                    copy.start()

    for copy in local[1:]:
        copy.wait()

    @pl.when(has_next)
    def _():
        for copy in halo_up:
            copy.wait_recv()

    @pl.when(has_prev)
    def _():
        for copy in halo_down:
            copy.wait_recv()

    lane = lax.broadcasted_iota(jnp.int32, (NZ, NY), 1)
    level = lax.broadcasted_iota(jnp.int32, (NZ, NY), 0)

    def above(v):
        return jnp.where(level < NZ - 1, pltpu.roll(v, NZ - 1, 0), 0.0)

    def below(v):
        return jnp.where(level > 0, pltpu.roll(v, 1, 0), 0.0)

    def right(v):
        return jnp.where(lane < NY - 1, pltpu.roll(v, NY - 1, 1), 0.0)

    def left(v):
        return jnp.where(lane > 0, pltpu.roll(v, 1, 1), 0.0)

    def plane_sum(v):
        return above(v) + below(v) + right(v) + left(v)

    def inside(i):
        at = place * R + i
        return jnp.logical_and(at >= 0, at < G * K * R)

    def voids_row(n, carry):
        v = 1.0 - cn[n].astype(jnp.float32) * particle_volume
        vo[n] = jnp.where(inside(n - H), v, 0.0)
        return carry

    lax.fori_loop(0, R + 2 * H, voids_row, 0)

    def weight_row(n, carry):
        v = vo[n]
        ws = 0.5 * (6.0 * v + vo[n - 1] + vo[n + 1] + plane_sum(v))
        rh[n] = jnp.where(inside(n - H), 1.0 / ws, 0.0)
        return carry

    lax.fori_loop(1, R + 2 * H - 1, weight_row, 0)

    for sender in range(G):
        spot = pl.ds(sender * W, W)
        here = {"gx": x, "gy": k}
        remote(z0.at[0, 0], u0.at[:, :, spot], s2_send.at[0], s2_recv.at[2 * sender], here).wait_recv()
        remote(z1.at[0, 0], u12.at[:, :, :, spot], s2_send.at[1], s2_recv.at[2 * sender + 1], here).wait_recv()

    def predict(i, u_of, force):
        v, va, vb = vo[H + i], vo[H + i - 1], vo[H + i + 1]
        ps = plane_sum(v)
        ws = 0.5 * (6.0 * v + va + vb + ps)
        u, ua, ub = u_of(i), u_of(i - 1), u_of(i + 1)
        near = ua + ub + plane_sum(u)
        nearv = va * ua + vb * ub + plane_sum(v * u)
        diffusion = 0.5 * (v * near + nearv) - ws * u
        drag = dr[i + 1]
        return (v * u + (time_step * viscosity) * diffusion + time_step * (drag * force)) / (v + time_step * drag)

    def first_row(n, carry):
        i = n - 1
        value = predict(i, lambda m: u0[m + 2], pv0[n])
        fl[n] = jnp.where(inside(i), vo[H + i] * value, 0.0)
        pred[0, n] = value
        return carry

    lax.fori_loop(0, R + 2, first_row, 0)

    def source_row(i, carry):
        v = vo[H + i]
        p1 = predict(i, lambda m: u12[0, m + 1], pv12[0, i])
        pred[1, i + 1] = p1
        f1 = v * p1
        p2 = predict(i, lambda m: u12[1, m + 1], pv12[1, i])
        pred[2, i + 1] = p2
        f2 = v * p2
        source = (fl[i + 2] - fl[i]) + (right(f1) - left(f1)) + (above(f2) - below(f2))
        b[H + i] = -source * rh[H + i]
        return carry

    lax.fori_loop(0, R, source_row, 0)

    def sweep(src, dst, reach):
        def row(n, carry):
            p, pa, pb = src[n], src[n - 1], src[n + 1]
            v, va, vb = vo[n], vo[n - 1], vo[n + 1]
            near = pa + pb + plane_sum(p)
            nearv = va * pa + vb * pb + plane_sum(v * p)
            dst[n] = (0.5 * (v * near + nearv)) * rh[n] + b[n]
            return carry

        lax.fori_loop(H - reach, H + R + reach, row, 0)

    def exchange(buf, turn, depth):
        upward = remote(buf.at[H:H + depth], buf.at[H + R:H + R + depth], pr_send.at[2 * turn], pr_recv.at[2 * turn], prev_id)
        downward = remote(
            buf.at[H + R - depth:H + R], buf.at[H - depth:H], pr_send.at[2 * turn + 1], pr_recv.at[2 * turn + 1], next_id
        )

        @pl.when(has_prev)
        def _():
            upward.start()

        @pl.when(has_next)
        def _():
            downward.start()

        @pl.when(has_next)
        def _():
            upward.wait_recv()

        @pl.when(has_prev)
        def _():
            downward.wait_recv()

        return upward, downward

    turn0 = exchange(b, 0, H)
    sweep(b, t0, 3)
    sweep(t0, t1, 2)
    sweep(t1, t0, 1)
    sweep(t0, pm, 0)
    turn1 = exchange(pm, 1, H)
    sweep(pm, t0, 3)
    sweep(t0, t1, 2)
    sweep(t1, pf, 1)

    home = x // C
    block = lax.rem(x, C) * K + k
    spot_rows = pl.ds(block * R, R)
    outs = []
    for e in range(G):
        target = lax.rem(x + e, G)
        src = pf.at[H:H + R, :, pl.ds(pl.multiple_of(target * W, W), W)]
        dst = po.at[spot_rows]
        far = remote(src, dst, out_send.at[e], out_recv.at[block], {"gx": target, "gy": home})
        if e == 0:
            near = pltpu.make_async_copy(src, dst, out_recv.at[block])

            @pl.when(home != k)
            def _(far=far):
                far.start()

            @pl.when(home == k)
            def _(near=near):
                near.start()
        else:
            far.start()
        outs.append(far)

    def slope_row(i, carry):
        n = H + i
        p = pf[n]
        g0 = 0.5 * (pf[n + 1] - pf[n - 1])
        g1 = 0.5 * (right(p) - left(p))
        g2 = 0.5 * (above(p) - below(p))
        for which, g in enumerate((g0, g1, g2)):
            grad_out[which, i] = g
            vel_out[which, i] = pred[which, i + 1] - time_step * g
        return carry

    lax.fori_loop(0, R, slope_row, 0)

    @pl.when(k > 0)
    def _():
        to_up.wait_send()

    @pl.when(k < K - 1)
    def _():
        to_down.wait_send()

    for pair in first:
        for copy in pair:
            copy.wait_send()
    for target, far0, far1 in second:
        @pl.when(target != x)
        def _(far0=far0, far1=far1):
            far0.wait_send()
            far1.wait_send()

    @pl.when(has_prev)
    def _():
        for copy in halo_up + [turn0[0], turn1[0]]:
            copy.wait_send()

    @pl.when(has_next)
    def _():
        for copy in halo_down + [turn0[1], turn1[1]]:
            copy.wait_send()

    for e, far in enumerate(outs):
        if e == 0:
            @pl.when(home != k)
            def _(far=far):
                far.wait_send()
        else:
            far.wait_send()

    for n in range(B):
        here = {"gx": x, "gy": k}
        remote(pf.at[H:H + R, :, 0:W], po.at[n * R:(n + 1) * R], out_send.at[0], out_recv.at[n], here).wait_recv()
    press_out[...] = po[...]


def shards(K, G, particle_count, drag_coeff, particle_velocity, fluid_velocity):
    NZ, R, NY = particle_count.shape
    rows, W = fluid_velocity.shape[2:]
    C = G // K
    H = ROUNDS[0]
    f32 = jnp.float32

    def turned(values):
        return jnp.swapaxes(values, -3, -2)

    dma = pltpu.SemaphoreType.DMA
    pad = (R + 2 * H, NZ, NY)
    scratch = [
        pltpu.VMEM((3, rows + 4, NZ, W), f32),
        pltpu.VMEM((K - 1, C, R + 4, NZ, W), f32),
        pltpu.VMEM((K - 1, C, 2, R + 2, NZ, W), f32),
        pltpu.VMEM((R + 4, NZ, NY), f32),
        pltpu.VMEM((2, R + 2, NZ, NY), f32),
        pltpu.VMEM(pad, jnp.int32),
        pltpu.VMEM((R + 2, NZ, NY), f32),
        pltpu.VMEM((R + 2, NZ, NY), f32),
        pltpu.VMEM((2, R, NZ, NY), f32),
        pltpu.VMEM(pad, f32),
        pltpu.VMEM(pad, f32),
        pltpu.VMEM((3, R + 2, NZ, NY), f32),
        pltpu.VMEM((R + 2, NZ, NY), f32),
        pltpu.VMEM(pad, f32),
        pltpu.VMEM(pad, f32),
        pltpu.VMEM(pad, f32),
        pltpu.VMEM(pad, f32),
        pltpu.VMEM(pad, f32),
        pltpu.VMEM((rows, NZ, W), f32),
        dma((5,)), dma((2,)), dma((2,)),
        dma(((K - 1) * C * 2,)), dma(((K - 1) * C * 2,)),
        dma((K * C * 2,)), dma((G * 2,)),
        dma((6,)), dma((6,)), dma((4,)), dma((4,)), dma((G,)), dma((C * K,)),
    ]
    vmem = pl.BlockSpec(memory_space=pltpu.VMEM)
    anywhere = pl.BlockSpec(memory_space=pl.ANY)
    pressure, velocity, slopes = pl.pallas_call(
        functools.partial(kernel, K, G, R, NZ, NY, W),
        out_shape=(
            jax.ShapeDtypeStruct((rows, NZ, W), f32),
            jax.ShapeDtypeStruct((3, R, NZ, NY), f32),
            jax.ShapeDtypeStruct((3, R, NZ, NY), f32),
        ),
        in_specs=[anywhere] * 4,
        out_specs=(vmem, vmem, vmem),
        scratch_shapes=scratch,
        compiler_params=pltpu.CompilerParams(has_side_effects=True, vmem_limit_bytes=48 * 1024 * 1024),
    )(turned(particle_count), turned(drag_coeff), turned(particle_velocity), turned(fluid_velocity))
    return turned(pressure), turned(velocity), turned(slopes)


def solution(mesh):
    placed = (
        P(None, ("gx", "gy"), None),
        P(None, ("gx", "gy"), None),
        P(None, None, ("gx", "gy"), None),
        P(None, None, "gy", "gx"),
    )
    return jax.shard_map(
        functools.partial(shards, mesh.shape["gy"], mesh.shape["gx"]),
        mesh=mesh,
        in_specs=placed,
        out_specs=(
            P(None, "gy", "gx"),
            P(None, None, ("gx", "gy"), None),
            P(None, None, ("gx", "gy"), None),
        ),
        check_vma=False,
    )
```

```python
import functools

import jax
import jax.numpy as jnp
from jax import lax
from jax.experimental import pallas as pl
from jax.experimental.pallas import tpu as pltpu
from jax.sharding import PartitionSpec as P

SWEEPS = 8
ROUNDS = (4, 4)

particle_volume = 0.05
time_step = 0.5
viscosity = 0.1


def kernel(
    K, G, R, NZ, NY, W,
    count_in, drag_in, pvel_in, fluid_in,
    press_out, vel_out, grad_out,
    fp, zb, ub, cn, dr, pv, vo, rh, pred, gr, fl, fr, t0, t1, pf, po,
    loc_sem, fh_send, fh_recv, s1_send, s1_recv, s2_send, s2_recv,
    hal_send, hal_recv, pr_send, pr_recv, out_send, out_recv, *stages,
):
    H = max(ROUNDS)
    b = stages[0]
    C = G // K
    B = C * K
    x = lax.axis_index("gx")
    k = lax.axis_index("gy")
    place = x * K + k
    has_prev = place > 0
    has_next = place < G * K - 1
    prev_id = {"gx": jnp.where(k > 0, x, jnp.maximum(x - 1, 0)), "gy": lax.rem(k + K - 1, K)}
    next_id = {"gx": jnp.where(k < K - 1, x, jnp.minimum(x + 1, G - 1)), "gy": lax.rem(k + 1, K)}

    def remote(src, dst, ssem, rsem, to):
        return pltpu.make_async_remote_copy(
            src_ref=src, dst_ref=dst, send_sem=ssem, recv_sem=rsem, device_id=to, device_id_type=pl.DeviceIdType.MESH
        )

    rows = R * B

    local = [[] for _ in range(4)]
    for z in range(NZ):
        local[0].append(pltpu.make_async_copy(fluid_in.at[:, z], fp.at[:, 1:rows + 1, z], loc_sem.at[z]))
        local[1].append(pltpu.make_async_copy(count_in.at[z], cn.at[H:H + R, z], loc_sem.at[NZ + z]))
        local[2].append(pltpu.make_async_copy(drag_in.at[z], dr.at[:, z], loc_sem.at[2 * NZ + z]))
        local[3].append(pltpu.make_async_copy(pvel_in.at[:, z], pv.at[:, :, z], loc_sem.at[3 * NZ + z]))
    for copies in local:
        for copy in copies:
            copy.start()

    home = x // C
    barrier = pltpu.get_barrier_semaphore()

    def greet(to):
        pl.semaphore_signal(barrier, inc=1, device_id=to, device_id_type=pl.DeviceIdType.MESH)

    for d in range(1, K):
        greet({"gx": x, "gy": lax.rem(k + d, K)})
    for e in range(1, G):
        greet({"gx": lax.rem(x + e, G), "gy": k})

    @pl.when(has_prev)
    def _():
        greet(prev_id)

    @pl.when(has_next)
    def _():
        greet(next_id)

    for c in range(C):
        for j in range(K):
            @pl.when(jnp.logical_or(k * C + c != x, k != j))
            def _(c=c, j=j):
                greet({"gx": k * C + c, "gy": jnp.int32(j)})

    one = jnp.int32(1)
    nothing = jnp.int32(0)
    heard = (
        K + G - 2 + G
        + jnp.where(has_prev, one, nothing)
        + jnp.where(has_next, one, nothing)
        - jnp.where(home == k, one, nothing)
    )

    @pl.when(k == 0)
    def _():
        fp[:, 0:1] = jnp.zeros((3, 1, NZ, W), jnp.float32)

    @pl.when(k == K - 1)
    def _():
        fp[:, rows + 1:rows + 2] = jnp.zeros((3, 1, NZ, W), jnp.float32)

    line = jnp.zeros((NZ, NY), jnp.float32)
    fl[0] = line
    fl[R + 1] = line
    edge = jnp.zeros((H, NZ, NY), jnp.float32)

    @pl.when(jnp.logical_not(has_prev))
    def _():
        fr[0] = line
        for buf in stages:
            buf[0:H] = edge

    @pl.when(jnp.logical_not(has_next))
    def _():
        fr[1] = line
        for buf in stages:
            buf[H + R:2 * H + R] = edge

    for copy in local[0]:
        copy.wait()
    pl.semaphore_wait(barrier, heard)

    up = {"gx": x, "gy": lax.rem(k + K - 1, K)}
    down = {"gx": x, "gy": lax.rem(k + 1, K)}
    to_up = remote(fp.at[:, 1:2], fp.at[:, rows + 1:rows + 2], fh_send.at[0], fh_recv.at[0], up)
    to_down = remote(fp.at[:, rows:rows + 1], fp.at[:, 0:1], fh_send.at[1], fh_recv.at[1], down)

    @pl.when(k > 0)
    def _():
        to_up.start()

    @pl.when(k < K - 1)
    def _():
        to_down.start()

    def part(at):
        return fp.at[:, pl.ds(at * R, R + 2)]

    def at_edge(c, j):
        low = (j == 0) if c == 0 else (j < 0)
        high = (j == K - 1) if c == C - 1 else (j < 0)
        return jnp.logical_or(low, high)

    columns = pl.ds(pl.multiple_of(x * W, W), W)

    def relay(d, c):
        source = lax.rem(k + K - d, K)
        target = source * C + c
        n = d * C + c
        src = part(c * K + k) if d == 0 else zb.at[d - 1, c]
        dst = ub.at[:, :, :, columns]
        far = remote(src, dst, s2_send.at[n], s2_recv.at[x], {"gx": target, "gy": k})
        near = pltpu.make_async_copy(src, dst, s2_recv.at[x])
        return target, far, near

    def pass_on(target, far, near):
        @pl.when(target != x)
        def _():
            far.start()

        @pl.when(target == x)
        def _():
            near.start()

    first = []
    for d in range(1, K):
        j = lax.rem(k + d, K)
        for c in range(C):
            n = (d - 1) * C + c
            first.append((c, j, remote(part(c * K + j), zb.at[d - 1, c], s1_send.at[n], s1_recv.at[n], {"gx": x, "gy": j})))
    second = [[relay(d, c) for c in range(C)] for d in range(K)]

    for c, j, copy in first:
        @pl.when(jnp.logical_not(at_edge(c, j)))
        def _(copy=copy):
            copy.start()

    for c in range(C):
        @pl.when(jnp.logical_not(at_edge(c, k)))
        def _(c=c):
            pass_on(*second[0][c])

    @pl.when(k < K - 1)
    def _():
        to_up.wait_recv()

    @pl.when(k > 0)
    def _():
        to_down.wait_recv()

    for c, j, copy in first:
        @pl.when(at_edge(c, j))
        def _(copy=copy):
            copy.start()

    for c in range(C):
        @pl.when(at_edge(c, k))
        def _(c=c):
            pass_on(*second[0][c])

    halo_up = [remote(cn.at[H:2 * H], cn.at[H + R:2 * H + R], hal_send.at[0], hal_recv.at[0], prev_id)]
    halo_down = [remote(cn.at[R:R + H], cn.at[0:H], hal_send.at[1], hal_recv.at[1], next_id)]

    for copies in local[1:]:
        for copy in copies:
            copy.wait()

    @pl.when(has_prev)
    def _():
        for copy in halo_up:
            copy.start()

    @pl.when(has_next)
    def _():
        for copy in halo_down:
            copy.start()

    for d in range(1, K):
        for c in range(C):
            first[(d - 1) * C + c][2].wait_recv()
            pass_on(*second[d][c])

    @pl.when(has_next)
    def _():
        for copy in halo_up:
            copy.wait_recv()

    @pl.when(has_prev)
    def _():
        for copy in halo_down:
            copy.wait_recv()

    lane = lax.broadcasted_iota(jnp.int32, (NZ, NY), 1)
    level = lax.broadcasted_iota(jnp.int32, (NZ, NY), 0)

    def above(v):
        return jnp.where(level < NZ - 1, pltpu.roll(v, NZ - 1, 0), 0.0)

    def below(v):
        return jnp.where(level > 0, pltpu.roll(v, 1, 0), 0.0)

    def right(v):
        return jnp.where(lane < NY - 1, pltpu.roll(v, NY - 1, 1), 0.0)

    def left(v):
        return jnp.where(lane > 0, pltpu.roll(v, 1, 1), 0.0)

    def plane_sum(v):
        return above(v) + below(v) + right(v) + left(v)

    def inside(i):
        at = place * R + i
        return jnp.logical_and(at >= 0, at < G * K * R)

    def voids_row(n, carry):
        v = 1.0 - cn[n].astype(jnp.float32) * particle_volume
        vo[n] = jnp.where(inside(n - H), v, 0.0)
        return carry

    lax.fori_loop(0, R + 2 * H, voids_row, 0)

    def weight_row(n, carry):
        v = vo[n]
        ws = 0.5 * (6.0 * v + vo[n - 1] + vo[n + 1] + plane_sum(v))
        rh[n] = jnp.where(inside(n - H), 1.0 / ws, 0.0)
        return carry

    lax.fori_loop(1, R + 2 * H - 1, weight_row, 0)

    for sender in range(G):
        spot = pl.ds(sender * W, W)
        here = {"gx": x, "gy": k}
        remote(zb.at[0, 0], ub.at[:, :, :, spot], s2_send.at[0], s2_recv.at[sender], here).wait_recv()

    def momentum_row(i, carry):
        v, va, vb = vo[H + i], vo[H + i - 1], vo[H + i + 1]
        ws = 0.5 * (6.0 * v + va + vb + plane_sum(v))
        drag = dr[i]
        below_line = 1.0 / (v + time_step * drag)
        for which in range(3):
            u, ua, ub_ = ub[which, i + 1], ub[which, i], ub[which, i + 2]
            near = ua + ub_ + plane_sum(u)
            nearv = va * ua + vb * ub_ + plane_sum(v * u)
            diffusion = 0.5 * (v * near + nearv) - ws * u
            force = drag * pv[which, i]
            value = (v * u + (time_step * viscosity) * diffusion + time_step * force) * below_line
            pred[which, i] = value
            f = v * value
            if which == 0:
                fl[i + 1] = f
            elif which == 1:
                part_source = right(f) - left(f)
            else:
                b[H + i] = part_source + (above(f) - below(f))
        return carry

    lax.fori_loop(0, R, momentum_row, 0)

    def source_row(i, carry):
        b[H + i] = -(fl[i + 2] - fl[i] + b[H + i]) * rh[H + i]
        return carry

    lax.fori_loop(0, R, source_row, 0)

    def sweep(src, dst, reach):
        def row(n, carry):
            p, pa, pb = src[n], src[n - 1], src[n + 1]
            v, va, vb = vo[n], vo[n - 1], vo[n + 1]
            near = pa + pb + plane_sum(p)
            nearv = va * pa + vb * pb + plane_sum(v * p)
            dst[n] = (0.5 * (v * near + nearv)) * rh[n] + b[n]
            return carry

        lax.fori_loop(H - reach, H + R + reach, row, 0)

    def exchange(turn, depth):
        buf = stages[turn]
        upward = [
            remote(buf.at[H:H + depth], buf.at[H + R:H + R + depth], pr_send.at[2 * turn], pr_recv.at[2 * turn], prev_id)
        ]
        downward = [
            remote(
                buf.at[H + R - depth:H + R], buf.at[H - depth:H], pr_send.at[2 * turn + 1], pr_recv.at[2 * turn + 1], next_id
            )
        ]
        if turn == 0:
            upward.append(remote(fl.at[1], fr.at[1], hal_send.at[2], hal_recv.at[2], prev_id))
            downward.append(remote(fl.at[R], fr.at[0], hal_send.at[3], hal_recv.at[3], next_id))

        @pl.when(has_prev)
        def _():
            for copy in upward:
                copy.start()

        @pl.when(has_next)
        def _():
            for copy in downward:
                copy.start()

        @pl.when(has_prev)
        def _():
            for copy in upward:
                copy.wait_send()

        @pl.when(has_next)
        def _():
            for copy in downward:
                copy.wait_send()

        @pl.when(has_next)
        def _():
            for copy in upward:
                copy.wait_recv()

        @pl.when(has_prev)
        def _():
            for copy in downward:
                copy.wait_recv()

    done = 0
    for turn, depth in enumerate(ROUNDS):
        exchange(turn, depth)
        if turn == 0:
            b[H] = b[H] + fr[0] * rh[H]
            b[H + R - 1] = b[H + R - 1] - fr[1] * rh[H + R - 1]
            b[H - 1] = b[H - 1] - fl[1] * rh[H - 1]
            b[H + R] = b[H + R] + fl[R] * rh[H + R]
        src = stages[turn]
        for reach in range(depth - 1, -1, -1):
            done += 1
            if done == SWEEPS:
                break
            if done == SWEEPS - 1:
                dst = pf
            elif reach == 0:
                dst = stages[turn + 1]
            else:
                dst = t1 if src is t0 else t0
            sweep(src, dst, reach)
            src = dst

    block = lax.rem(x, C) * K + k
    spot_rows = pl.ds(block * R, R)
    outs = []
    for e in range(G):
        target = lax.rem(x + e, G)
        src = pf.at[H:H + R, :, pl.ds(pl.multiple_of(target * W, W), W)]
        dst = po.at[spot_rows]
        far = remote(src, dst, out_send.at[e], out_recv.at[block], {"gx": target, "gy": home})
        if e == 0:
            near = pltpu.make_async_copy(src, dst, out_recv.at[block])

            @pl.when(home != k)
            def _(far=far):
                far.start()

            @pl.when(home == k)
            def _(near=near):
                near.start()
        else:
            far.start()
        outs.append(far)

    def slope_row(i, carry):
        n = H + i
        p = pf[n]
        g0 = 0.5 * (pf[n + 1] - pf[n - 1])
        g1 = 0.5 * (right(p) - left(p))
        g2 = 0.5 * (above(p) - below(p))
        for which, g in enumerate((g0, g1, g2)):
            gr[which, i] = g
            pred[which, i] = pred[which, i] - time_step * g
        return carry

    lax.fori_loop(0, R, slope_row, 0)
    written = []
    for z in range(NZ):
        written.append(pltpu.make_async_copy(gr.at[:, :, z], grad_out.at[:, z], loc_sem.at[z]))
        written.append(pltpu.make_async_copy(pred.at[:, :, z], vel_out.at[:, z], loc_sem.at[NZ + z]))
    for copy in written:
        copy.start()

    @pl.when(k > 0)
    def _():
        to_up.wait_send()

    @pl.when(k < K - 1)
    def _():
        to_down.wait_send()

    for c, j, copy in first:
        copy.wait_send()
    for pair in second:
        for target, far, near in pair:
            @pl.when(target != x)
            def _(far=far):
                far.wait_send()

    @pl.when(has_prev)
    def _():
        for copy in halo_up:
            copy.wait_send()

    @pl.when(has_next)
    def _():
        for copy in halo_down:
            copy.wait_send()

    for e, far in enumerate(outs):
        if e == 0:
            @pl.when(home != k)
            def _(far=far):
                far.wait_send()
        else:
            far.wait_send()

    for n in range(B):
        here = {"gx": x, "gy": k}
        remote(pf.at[H:H + R, :, 0:W], po.at[n * R:(n + 1) * R], out_send.at[0], out_recv.at[n], here).wait_recv()
    last = [pltpu.make_async_copy(po.at[:, z], press_out.at[z], loc_sem.at[2 * NZ + z]) for z in range(NZ)]
    for copy in last:
        copy.start()
    for copy in written + last:
        copy.wait()


def shards(K, G, particle_count, drag_coeff, particle_velocity, fluid_velocity):
    NZ, R, NY = particle_count.shape
    rows, W = fluid_velocity.shape[2:]
    C = G // K
    H = max(ROUNDS)
    f32 = jnp.float32

    dma = pltpu.SemaphoreType.DMA
    pad = (R + 2 * H, NZ, NY)
    scratch = [
        pltpu.VMEM((3, rows + 2, NZ, W), f32),
        pltpu.VMEM((K - 1, C, 3, R + 2, NZ, W), f32),
        pltpu.VMEM((3, R + 2, NZ, NY), f32),
        pltpu.VMEM(pad, jnp.int32),
        pltpu.VMEM((R, NZ, NY), f32),
        pltpu.VMEM((3, R, NZ, NY), f32),
        pltpu.VMEM(pad, f32),
        pltpu.VMEM(pad, f32),
        pltpu.VMEM((3, R, NZ, NY), f32),
        pltpu.VMEM((3, R, NZ, NY), f32),
        pltpu.VMEM((R + 2, NZ, NY), f32),
        pltpu.VMEM((2, NZ, NY), f32),
        pltpu.VMEM(pad, f32),
        pltpu.VMEM(pad, f32),
        pltpu.VMEM(pad, f32),
        pltpu.VMEM((rows, NZ, W), f32),
        dma((4 * NZ,)), dma((2,)), dma((2,)),
        dma(((K - 1) * C,)), dma(((K - 1) * C,)),
        dma((K * C,)), dma((G,)),
        dma((4,)), dma((4,)), dma((2 * len(ROUNDS),)), dma((2 * len(ROUNDS),)), dma((G,)), dma((C * K,)),
        *[pltpu.VMEM(pad, f32) for _ in ROUNDS],
    ]
    anywhere = pl.BlockSpec(memory_space=pl.ANY)
    return pl.pallas_call(
        functools.partial(kernel, K, G, R, NZ, NY, W),
        out_shape=(
            jax.ShapeDtypeStruct((NZ, rows, W), f32),
            jax.ShapeDtypeStruct((3, NZ, R, NY), f32),
            jax.ShapeDtypeStruct((3, NZ, R, NY), f32),
        ),
        in_specs=[anywhere] * 4,
        out_specs=(anywhere, anywhere, anywhere),
        scratch_shapes=scratch,
        compiler_params=pltpu.CompilerParams(collective_id=0, has_side_effects=True, vmem_limit_bytes=48 * 1024 * 1024),
    )(particle_count, drag_coeff, particle_velocity, fluid_velocity)


def solution(mesh):
    placed = (
        P(None, ("gx", "gy"), None),
        P(None, ("gx", "gy"), None),
        P(None, None, ("gx", "gy"), None),
        P(None, None, "gy", "gx"),
    )
    return jax.shard_map(
        functools.partial(shards, mesh.shape["gy"], mesh.shape["gx"]),
        mesh=mesh,
        in_specs=placed,
        out_specs=(
            P(None, "gy", "gx"),
            P(None, None, ("gx", "gy"), None),
            P(None, None, ("gx", "gy"), None),
        ),
        check_vma=False,
    )
```

```python
import functools

import jax
import jax.numpy as jnp
from jax import lax
from jax.experimental import pallas as pl
from jax.experimental.pallas import tpu as pltpu
from jax.sharding import PartitionSpec as P

SWEEPS = 8
ROUNDS = (4, 4)

particle_volume = 0.05
time_step = 0.5
viscosity = 0.1


def kernel(
    K, G, R, NZ, NY, W,
    count_in, drag_in, pvel_in, fluid_in,
    press_out, vel_out, grad_out,
    fp, ub, cn, dr, pv, vo, total_w, wf, wr, wa, rh, pred, gr, fl, fr, t0, t1, pf, po,
    loc_sem, fh_send, fh_recv, s2_send, s2_recv,
    hal_send, hal_recv, pr_send, pr_recv, out_send, out_recv, *stages,
):
    H = max(ROUNDS)
    b = stages[0]
    C = G // K
    B = C * K
    x = lax.axis_index("gx")
    k = lax.axis_index("gy")
    place = x * K + k
    has_prev = place > 0
    has_next = place < G * K - 1
    prev_id = {"gx": jnp.where(k > 0, x, jnp.maximum(x - 1, 0)), "gy": lax.rem(k + K - 1, K)}
    next_id = {"gx": jnp.where(k < K - 1, x, jnp.minimum(x + 1, G - 1)), "gy": lax.rem(k + 1, K)}

    def remote(src, dst, ssem, rsem, to):
        return pltpu.make_async_remote_copy(
            src_ref=src, dst_ref=dst, send_sem=ssem, recv_sem=rsem, device_id=to, device_id_type=pl.DeviceIdType.MESH
        )

    rows = R * B

    local = [[] for _ in range(4)]
    for z in range(NZ):
        local[0].append(pltpu.make_async_copy(fluid_in.at[:, z], fp.at[:, 1:rows + 1, z], loc_sem.at[z]))
        local[1].append(pltpu.make_async_copy(count_in.at[z], cn.at[H:H + R, z], loc_sem.at[NZ + z]))
        local[2].append(pltpu.make_async_copy(drag_in.at[z], dr.at[:, z], loc_sem.at[2 * NZ + z]))
        local[3].append(pltpu.make_async_copy(pvel_in.at[:, z], pv.at[:, :, z], loc_sem.at[3 * NZ + z]))
    for copies in local:
        for copy in copies:
            copy.start()

    home = x // C
    barrier = pltpu.get_barrier_semaphore()

    def greet(to):
        pl.semaphore_signal(barrier, inc=1, device_id=to, device_id_type=pl.DeviceIdType.MESH)

    for d in range(1, K):
        greet({"gx": x, "gy": lax.rem(k + d, K)})
    @pl.when(has_prev)
    def _():
        greet(prev_id)

    @pl.when(has_next)
    def _():
        greet(next_id)

    for c in range(C):
        for j in range(K):
            @pl.when(jnp.logical_or(k * C + c != x, k != j))
            def _(c=c, j=j):
                greet({"gx": k * C + c, "gy": jnp.int32(j)})

    for t in range(G):
        @pl.when(jnp.logical_or(home != k, x != t))
        def _(t=t):
            greet({"gx": jnp.int32(t), "gy": home})

    one = jnp.int32(1)
    nothing = jnp.int32(0)
    heard = (
        K - 1 + G + C * K
        + jnp.where(has_prev, one, nothing)
        + jnp.where(has_next, one, nothing)
        - 2 * jnp.where(home == k, one, nothing)
    )

    @pl.when(k == 0)
    def _():
        fp[:, 0:1] = jnp.zeros((3, 1, NZ, W), jnp.float32)

    @pl.when(k == K - 1)
    def _():
        fp[:, rows + 1:rows + 2] = jnp.zeros((3, 1, NZ, W), jnp.float32)

    line = jnp.zeros((NZ, NY), jnp.float32)
    fl[0] = line
    fl[R + 1] = line
    edge = jnp.zeros((H, NZ, NY), jnp.float32)

    @pl.when(jnp.logical_not(has_prev))
    def _():
        fr[0] = line
        for buf in stages:
            buf[0:H] = edge

    @pl.when(jnp.logical_not(has_next))
    def _():
        fr[1] = line
        for buf in stages:
            buf[H + R:2 * H + R] = edge

    for copy in local[0]:
        copy.wait()
    pl.semaphore_wait(barrier, heard)

    up = {"gx": x, "gy": lax.rem(k + K - 1, K)}
    down = {"gx": x, "gy": lax.rem(k + 1, K)}
    to_up = remote(fp.at[:, 1:2], fp.at[:, rows + 1:rows + 2], fh_send.at[0], fh_recv.at[0], up)
    to_down = remote(fp.at[:, rows:rows + 1], fp.at[:, 0:1], fh_send.at[1], fh_recv.at[1], down)

    @pl.when(k > 0)
    def _():
        to_up.start()

    @pl.when(k < K - 1)
    def _():
        to_down.start()

    def part(at):
        return fp.at[:, pl.ds(at * R, R + 2)]

    def at_edge(c, j):
        low = (j == 0) if c == 0 else (j < 0)
        high = (j == K - 1) if c == C - 1 else (j < 0)
        return jnp.logical_or(low, high)

    columns = pl.ds(pl.multiple_of(x * W, W), W)

    sends = []
    for d in range(K):
        for c in range(C):
            j = lax.rem(k + d, K)
            target = k * C + c
            src = part(c * K + j)
            dst = ub.at[:, :, :, columns]
            far = remote(src, dst, s2_send.at[d * C + c], s2_recv.at[x], {"gx": target, "gy": j})
            near = pltpu.make_async_copy(src, dst, s2_recv.at[x])
            sends.append((c, j, far, near, jnp.logical_and(target == x, j == k)))

    def send_all(edges):
        for c, j, far, near, mine in sends:
            want = at_edge(c, j) if edges else jnp.logical_not(at_edge(c, j))

            @pl.when(jnp.logical_and(want, mine))
            def _(near=near):
                near.start()

            @pl.when(jnp.logical_and(want, jnp.logical_not(mine)))
            def _(far=far):
                far.start()

    send_all(False)

    @pl.when(k < K - 1)
    def _():
        to_up.wait_recv()

    @pl.when(k > 0)
    def _():
        to_down.wait_recv()

    send_all(True)

    halo_up = [remote(cn.at[H:2 * H], cn.at[H + R:2 * H + R], hal_send.at[0], hal_recv.at[0], prev_id)]
    halo_down = [remote(cn.at[R:R + H], cn.at[0:H], hal_send.at[1], hal_recv.at[1], next_id)]

    for copies in local[1:]:
        for copy in copies:
            copy.wait()

    @pl.when(has_prev)
    def _():
        for copy in halo_up:
            copy.start()

    @pl.when(has_next)
    def _():
        for copy in halo_down:
            copy.start()

    @pl.when(has_next)
    def _():
        for copy in halo_up:
            copy.wait_recv()

    @pl.when(has_prev)
    def _():
        for copy in halo_down:
            copy.wait_recv()

    lane = lax.broadcasted_iota(jnp.int32, (NZ, NY), 1)
    level = lax.broadcasted_iota(jnp.int32, (NZ, NY), 0)

    def above(v):
        return jnp.where(level < NZ - 1, pltpu.roll(v, NZ - 1, 0), 0.0)

    def below(v):
        return jnp.where(level > 0, pltpu.roll(v, 1, 0), 0.0)

    def right(v):
        return jnp.where(lane < NY - 1, pltpu.roll(v, NY - 1, 1), 0.0)

    def left(v):
        return jnp.where(lane > 0, pltpu.roll(v, 1, 1), 0.0)

    def plane_sum(v):
        return above(v) + below(v) + right(v) + left(v)

    def inside(i):
        at = place * R + i
        return jnp.logical_and(at >= 0, at < G * K * R)

    def voids_row(n, carry):
        v = 1.0 - cn[n].astype(jnp.float32) * particle_volume
        vo[n] = jnp.where(inside(n - H), v, 0.0)
        return carry

    lax.fori_loop(0, R + 2 * H, voids_row, 0)

    def weight_row(n, carry):
        v = vo[n]
        ws = 0.5 * (6.0 * v + vo[n - 1] + vo[n + 1] + plane_sum(v))
        total_w[n] = ws
        rh[n] = jnp.where(inside(n - H), 1.0 / ws, 0.0)
        wf[n] = 0.5 * (v + vo[n + 1])
        wr[n] = jnp.where(lane < NY - 1, 0.5 * (v + pltpu.roll(v, NY - 1, 1)), 0.0)
        wa[n] = jnp.where(level < NZ - 1, 0.5 * (v + pltpu.roll(v, NZ - 1, 0)), 0.0)
        return carry

    wf[0] = 0.5 * (vo[0] + vo[1])
    lax.fori_loop(1, R + 2 * H - 1, weight_row, 0)

    def weighted(n, p, pa, pb):
        r, a = wr[n], wa[n]
        across = r * pltpu.roll(p, NY - 1, 1) + pltpu.roll(r * p, 1, 1)
        upright = a * pltpu.roll(p, NZ - 1, 0) + pltpu.roll(a * p, 1, 0)
        return (wf[n - 1] * pa + wf[n] * pb) + (across + upright)

    for sender in range(G):
        spot = pl.ds(sender * W, W)
        here = {"gx": x, "gy": k}
        remote(part(0), ub.at[:, :, :, spot], s2_send.at[0], s2_recv.at[sender], here).wait_recv()

    def momentum_row(i, carry):
        v, ws = vo[H + i], total_w[H + i]
        drag = dr[i]
        below_line = 1.0 / (v + time_step * drag)
        for which in range(3):
            u = ub[which, i + 1]
            diffusion = weighted(H + i, u, ub[which, i], ub[which, i + 2]) - ws * u
            force = drag * pv[which, i]
            value = (v * u + (time_step * viscosity) * diffusion + time_step * force) * below_line
            pred[which, i] = value
            f = v * value
            if which == 0:
                fl[i + 1] = f
            elif which == 1:
                part_source = right(f) - left(f)
            else:
                b[H + i] = part_source + (above(f) - below(f))
        return carry

    lax.fori_loop(0, R, momentum_row, 0)

    def source_row(i, carry):
        b[H + i] = -(fl[i + 2] - fl[i] + b[H + i]) * rh[H + i]
        return carry

    lax.fori_loop(0, R, source_row, 0)

    def sweep(src, dst, reach):
        def row(n, carry):
            dst[n] = weighted(n, src[n], src[n - 1], src[n + 1]) * rh[n] + b[n]
            return carry

        lax.fori_loop(H - reach, H + R + reach, row, 0)

    def exchange(turn, depth):
        buf = stages[turn]
        upward = [
            remote(buf.at[H:H + depth], buf.at[H + R:H + R + depth], pr_send.at[2 * turn], pr_recv.at[2 * turn], prev_id)
        ]
        downward = [
            remote(
                buf.at[H + R - depth:H + R], buf.at[H - depth:H], pr_send.at[2 * turn + 1], pr_recv.at[2 * turn + 1], next_id
            )
        ]
        if turn == 0:
            upward.append(remote(fl.at[1], fr.at[1], hal_send.at[2], hal_recv.at[2], prev_id))
            downward.append(remote(fl.at[R], fr.at[0], hal_send.at[3], hal_recv.at[3], next_id))

        @pl.when(has_prev)
        def _():
            for copy in upward:
                copy.start()

        @pl.when(has_next)
        def _():
            for copy in downward:
                copy.start()

        @pl.when(has_prev)
        def _():
            for copy in upward:
                copy.wait_send()

        @pl.when(has_next)
        def _():
            for copy in downward:
                copy.wait_send()

        @pl.when(has_next)
        def _():
            for copy in upward:
                copy.wait_recv()

        @pl.when(has_prev)
        def _():
            for copy in downward:
                copy.wait_recv()

    done = 0
    for turn, depth in enumerate(ROUNDS):
        exchange(turn, depth)
        if turn == 0:
            b[H] = b[H] + fr[0] * rh[H]
            b[H + R - 1] = b[H + R - 1] - fr[1] * rh[H + R - 1]
            b[H - 1] = b[H - 1] - fl[1] * rh[H - 1]
            b[H + R] = b[H + R] + fl[R] * rh[H + R]
        src = stages[turn]
        for reach in range(depth - 1, -1, -1):
            done += 1
            if done == SWEEPS:
                break
            if done == SWEEPS - 1:
                dst = pf
            elif reach == 0:
                dst = stages[turn + 1]
            else:
                dst = t1 if src is t0 else t0
            sweep(src, dst, reach)
            src = dst

    block = lax.rem(x, C) * K + k
    spot_rows = pl.ds(block * R, R)
    outs = []
    for e in range(G):
        target = lax.rem(x + e, G)
        src = pf.at[H:H + R, :, pl.ds(pl.multiple_of(target * W, W), W)]
        dst = po.at[spot_rows]
        far = remote(src, dst, out_send.at[e], out_recv.at[block], {"gx": target, "gy": home})
        if e == 0:
            near = pltpu.make_async_copy(src, dst, out_recv.at[block])

            @pl.when(home != k)
            def _(far=far):
                far.start()

            @pl.when(home == k)
            def _(near=near):
                near.start()
        else:
            far.start()
        outs.append(far)

    def slope_row(i, carry):
        n = H + i
        p = pf[n]
        g0 = 0.5 * (pf[n + 1] - pf[n - 1])
        g1 = 0.5 * (right(p) - left(p))
        g2 = 0.5 * (above(p) - below(p))
        for which, g in enumerate((g0, g1, g2)):
            gr[which, i] = g
            pred[which, i] = pred[which, i] - time_step * g
        return carry

    lax.fori_loop(0, R, slope_row, 0)
    written = []
    for z in range(NZ):
        written.append(pltpu.make_async_copy(gr.at[:, :, z], grad_out.at[:, z], loc_sem.at[z]))
        written.append(pltpu.make_async_copy(pred.at[:, :, z], vel_out.at[:, z], loc_sem.at[NZ + z]))
    for copy in written:
        copy.start()

    @pl.when(k > 0)
    def _():
        to_up.wait_send()

    @pl.when(k < K - 1)
    def _():
        to_down.wait_send()

    for c, j, far, near, mine in sends:
        @pl.when(jnp.logical_not(mine))
        def _(far=far):
            far.wait_send()

    @pl.when(has_prev)
    def _():
        for copy in halo_up:
            copy.wait_send()

    @pl.when(has_next)
    def _():
        for copy in halo_down:
            copy.wait_send()

    for e, far in enumerate(outs):
        if e == 0:
            @pl.when(home != k)
            def _(far=far):
                far.wait_send()
        else:
            far.wait_send()

    for n in range(B):
        here = {"gx": x, "gy": k}
        remote(pf.at[H:H + R, :, 0:W], po.at[n * R:(n + 1) * R], out_send.at[0], out_recv.at[n], here).wait_recv()
    last = [pltpu.make_async_copy(po.at[:, z], press_out.at[z], loc_sem.at[2 * NZ + z]) for z in range(NZ)]
    for copy in last:
        copy.start()
    for copy in written + last:
        copy.wait()


def shards(K, G, particle_count, drag_coeff, particle_velocity, fluid_velocity):
    NZ, R, NY = particle_count.shape
    rows, W = fluid_velocity.shape[2:]
    C = G // K
    H = max(ROUNDS)
    f32 = jnp.float32

    dma = pltpu.SemaphoreType.DMA
    pad = (R + 2 * H, NZ, NY)
    scratch = [
        pltpu.VMEM((3, rows + 2, NZ, W), f32),
        pltpu.VMEM((3, R + 2, NZ, NY), f32),
        pltpu.VMEM(pad, jnp.int32),
        pltpu.VMEM((R, NZ, NY), f32),
        pltpu.VMEM((3, R, NZ, NY), f32),
        *[pltpu.VMEM(pad, f32) for _ in range(6)],
        pltpu.VMEM((3, R, NZ, NY), f32),
        pltpu.VMEM((3, R, NZ, NY), f32),
        pltpu.VMEM((R + 2, NZ, NY), f32),
        pltpu.VMEM((2, NZ, NY), f32),
        pltpu.VMEM(pad, f32),
        pltpu.VMEM(pad, f32),
        pltpu.VMEM(pad, f32),
        pltpu.VMEM((rows, NZ, W), f32),
        dma((4 * NZ,)), dma((2,)), dma((2,)),
        dma((K * C,)), dma((G,)),
        dma((4,)), dma((4,)), dma((2 * len(ROUNDS),)), dma((2 * len(ROUNDS),)), dma((G,)), dma((C * K,)),
        *[pltpu.VMEM(pad, f32) for _ in ROUNDS],
    ]
    anywhere = pl.BlockSpec(memory_space=pl.ANY)
    return pl.pallas_call(
        functools.partial(kernel, K, G, R, NZ, NY, W),
        out_shape=(
            jax.ShapeDtypeStruct((NZ, rows, W), f32),
            jax.ShapeDtypeStruct((3, NZ, R, NY), f32),
            jax.ShapeDtypeStruct((3, NZ, R, NY), f32),
        ),
        in_specs=[anywhere] * 4,
        out_specs=(anywhere, anywhere, anywhere),
        scratch_shapes=scratch,
        compiler_params=pltpu.CompilerParams(collective_id=0, has_side_effects=True, vmem_limit_bytes=67043328),
    )(particle_count, drag_coeff, particle_velocity, fluid_velocity)


def solution(mesh):
    placed = (
        P(None, ("gx", "gy"), None),
        P(None, ("gx", "gy"), None),
        P(None, None, ("gx", "gy"), None),
        P(None, None, "gy", "gx"),
    )
    return jax.shard_map(
        functools.partial(shards, mesh.shape["gy"], mesh.shape["gx"]),
        mesh=mesh,
        in_specs=placed,
        out_specs=(
            P(None, "gy", "gx"),
            P(None, None, ("gx", "gy"), None),
            P(None, None, ("gx", "gy"), None),
        ),
        check_vma=False,
    )
```
